512 devices in a mesh: fsdp: 32 (over z_lo, y), tp: 16 (over z_hi, x, core).
Axes of the slice: x: 4, y: 4, z: 16 (z_hi: 2, z_lo: 8; z = z_hi * 8 + z_lo), core: 2. Of those that a mesh axis runs over, the one named last changes fastest.
Arguments:
- base_weight: bfloat16 [16384, 26624], P(('fsdp', 'tp')), may hold values from -0.1875 to 0.1875
- left_factor: bfloat16 [16384, 64], P(('fsdp', 'tp')), may hold values from -0.75 to 0.75
- right_factor: bfloat16 [64, 26624], P(None, 'tp'), may hold values from -0.029907227 to 0.029907227
- magnitude: float32 [26624], replicated, may hold values from 6 to 96
Outputs:
- quantized: bfloat16 [16384, 26624], P('fsdp', 'tp')
- block_scales: float32 [128, 208], P('fsdp', 'tp')
The draws below stay inside these ranges and needn't reach their ends.
All inputs are finite; a program needn't handle non-finite values. Where the reference program divides by a largest or mean magnitude, that divisor is 1e-20 or more.
Results may differ from the reference program's by a relative error of at most 0.01.
Values may be sent and summed in bfloat16 or wider, within the bound.
A program may use at most 64 MiB of HBM per device.

```python
import math
import jax
import jax.numpy as jnp
from jax import lax

DIN = 16384
DOUT = 26624
RANK = 64
BLOCK = 128


def spiked(result, own_key, source, target, shards_of, factor):
    def block_of(position):
        return (jnp.arange(result.shape[position]) // (result.shape[position] // shards_of)).reshape((-1,) + (1,) * (result.ndim - 1 - position))

    one_side = jax.random.permutation(own_key, shards_of)[block_of(target)]
    other_side = (block_of(target) + shards_of // 2) % shards_of
    return jnp.where((block_of(source) == one_side) | (block_of(source) == other_side), factor * result, result)


def steps_of(own_key, dims, cuts, low, high):
    def one(dim, blocks):
        steps = jax.random.uniform(jax.random.fold_in(jax.random.fold_in(own_key, 6), dim), (blocks,), jnp.float32, low / len(cuts), high / len(cuts))
        return jnp.repeat(jnp.exp(steps), dims[dim] // blocks).reshape((-1,) + (1,) * (len(dims) - dim - 1))

    gain = one(*cuts[0])
    for cut in cuts[1:]:
        gain = gain * one(*cut)
    return gain


def noise(key, dims, deviation, most, split=(), kind=jnp.bfloat16):
    values = jax.random.normal(key, dims, jnp.float32) * deviation
    if len(split) > 0:
        values = steps_of(key, dims, split, -0.22, 0.18) * values
    return jnp.clip(values, min=-most, max=most).astype(kind)


def noise_with(rng, dims, scale, bound, pieces, heavy, kind=jnp.bfloat16):
    entries = scale * jax.random.normal(rng, dims, jnp.float32)
    if pieces:
        entries = entries * steps_of(rng, dims, pieces, -0.22, 0.18)
    return jnp.clip(spiked(entries, jax.random.fold_in(rng, 3), *heavy), -bound, bound).astype(kind)


def setup_inputs(seed: int = 0) -> dict:
    key_of = jax.random.split(jax.random.key(seed), 5)
    return {
        "base_weight": noise_with(key_of[0], (DIN, DOUT), DIN ** -0.5, 0.1875, ((0, 512),), (0, 1, 512, 6.0)),
        "left_factor": noise(key_of[1], (DIN, RANK), RANK ** -0.5, 0.75, ((0, 512),)),
        "right_factor": noise(key_of[2], (RANK, DOUT), 0.005, 0.029907227, ((1, 16),)),
        "magnitude": jnp.clip(jnp.exp(jax.random.uniform(key_of[3], (DOUT,), jnp.float32, math.log(6.0), math.log(96.0))), 6.0, 96.0),
    }


epsilon = 1e-06

def reference(base_weight, left_factor, right_factor, magnitude):
    block_total = DOUT // BLOCK

    def one_block(block_index):
        start = (block_index * BLOCK).astype(jnp.int32)
        base_cols = lax.dynamic_slice_in_dim(base_weight, start, BLOCK, 1)
        right_cols = lax.dynamic_slice_in_dim(right_factor, start, BLOCK, 1)
        mag_cols = lax.dynamic_slice_in_dim(magnitude, start, BLOCK, 0)
        combined = base_cols.astype(jnp.float32) + jnp.dot(left_factor, right_cols, preferred_element_type=jnp.float32)
        col_norm = jnp.sqrt(lax.optimization_barrier(jnp.sum(combined * combined, axis=0)) + epsilon)
        merged = (mag_cols * combined / col_norm).astype(jnp.bfloat16)
        tile_view = merged.astype(jnp.float32).reshape(DIN // BLOCK, BLOCK, BLOCK)
        block_max = lax.optimization_barrier(jnp.max(jnp.abs(tile_view), axis=(1, 2)))
        scaled = (tile_view / (block_max[:, None, None] + epsilon)).reshape(DIN, BLOCK).astype(jnp.bfloat16)
        return (scaled, block_max)
    scaled_all, max_all = lax.map(one_block, jnp.arange(block_total, dtype=jnp.int32))
    quantized = jnp.transpose(scaled_all, (1, 0, 2)).reshape(DIN, DOUT)
    block_scales = jnp.transpose(max_all, (1, 0))
    return (quantized, block_scales)
```

```python
import functools

import jax
import jax.numpy as jnp
from jax import lax
from jax.experimental import pallas as pl
from jax.experimental.pallas import tpu as pltpu
from jax.sharding import PartitionSpec as P

MESH = pl.DeviceIdType.MESH
BLOCK = 128
EPS = 1e-06
NB = (5, 4, 4)
C0 = (0, 5, 9)
ROWS = 32
COLS = 1664
NX = 4
NY = 4
NZ = 16
HOPS = 8
PLANE = 8


def kernel(w, lf, rf, mag, out, scales, wall, rb, ball, rbb, rfv, magv, comb, outv, *refs):
    psy, psz = refs[:3], refs[3:6]
    scv, ring_s, ring_r, bring_s, bring_r, pl_s, st_r, own_r, bp_s, bp_r, y_s, y_r, z_s, z_r, loc, outs = refs[6:]
    f, t = lax.axis_index("fsdp"), lax.axis_index("tp")
    zlo, y = f // NY, lax.rem(f, NY)
    half, x, core = t // PLANE, lax.rem(t, PLANE) // 2, lax.rem(t, 2)
    z = half * 8 + zlo
    me = x * 2 + core

    def dev(zz, yy, k):
        return (lax.rem(zz, 8) * NY + yy, (zz // 8) * PLANE + k)

    z_up, z_dn = lax.rem(z + 1, NZ), lax.rem(z + NZ - 1, NZ)
    up, dn = dev(z_up, y, me), dev(z_dn, y, me)
    plane = [lax.rem(x + dx, NX) * 2 + lax.rem(core + dc, 2) for dx in (0, 1, 3, 2) for dc in (0, 1)][1:]
    y_peers = [lax.rem(y + d, NY) for d in range(1, NY)]
    z_peers = [lax.rem(zlo + d, 8) for d in range(1, 8)]

    loads = [
        pltpu.make_async_copy(rf, rfv, loc.at[0]),
        pltpu.make_async_copy(mag, magv, loc.at[1]),
        pltpu.make_async_copy(lf, ball.at[pl.ds(pl.multiple_of(t * ROWS, ROWS), ROWS), :], loc.at[2]),
        pltpu.make_async_copy(
            w.at[:, pl.ds(pl.multiple_of(t * COLS, BLOCK), COLS)],
            wall.at[pl.ds(pl.multiple_of(t * ROWS, ROWS), ROWS), :],
            loc.at[3],
        ),
    ]
    far = (1 - half) * PLANE
    own_stage = pltpu.make_async_copy(
        w.at[:, pl.ds(pl.multiple_of((far + me) * COLS, BLOCK), COLS)],
        rb.at[0, pl.ds(pl.multiple_of(me * ROWS, ROWS), ROWS), :],
        loc.at[4],
    )
    own_stage.start()
    for c in loads:
        c.start()

    barrier = pltpu.get_barrier_semaphore()
    peers = [up, dn] + [dev(z, y, k) for k in plane] + [dev(z, q, me) for q in y_peers]
    peers += [dev(half * 8 + q, y, me) for q in z_peers]
    for p in peers:
        pl.semaphore_signal(barrier, inc=1, device_id=p, device_id_type=MESH)
    pl.semaphore_wait(barrier, len(peers))

    def cols(b):
        return pl.ds(C0[b] * BLOCK, NB[b] * BLOCK)

    def stage_copy(b, i):
        k = plane[i]
        return pltpu.make_async_remote_copy(
            w.at[:, pl.ds(pl.multiple_of((far + k) * COLS + C0[b] * BLOCK, BLOCK), NB[b] * BLOCK)],
            rb.at[0, pl.ds(pl.multiple_of(me * ROWS, ROWS), ROWS), cols(b)],
            pl_s.at[0],
            st_r.at[b, me],
            device_id=dev(z, y, k),
            device_id_type=MESH,
        )

    def stage_wait(b, k):
        pltpu.make_async_remote_copy(
            rb.at[0, pl.ds(pl.multiple_of(k * ROWS, ROWS), ROWS), cols(b)],
            rb.at[0, pl.ds(pl.multiple_of(k * ROWS, ROWS), ROWS), cols(b)],
            pl_s.at[0],
            st_r.at[b, k],
            device_id=dev(z, y, k),
            device_id_type=MESH,
        ).wait_recv()

    def own_copy(i):
        k = plane[i]
        return pltpu.make_async_remote_copy(
            w.at[:, pl.ds(pl.multiple_of((half * PLANE + k) * COLS, BLOCK), COLS)],
            wall.at[pl.ds(pl.multiple_of(t * ROWS, ROWS), ROWS), :],
            pl_s.at[0],
            own_r.at[me],
            device_id=dev(z, y, k),
            device_id_type=MESH,
        )

    def own_wait(k):
        row = pl.ds(pl.multiple_of((half * PLANE + k) * ROWS, ROWS), ROWS)
        pltpu.make_async_remote_copy(
            wall.at[row, :], wall.at[row, :], pl_s.at[0], own_r.at[k], device_id=dev(z, y, k), device_id_type=MESH
        ).wait_recv()

    def ring_copy(b, s, k, d):
        row = pl.ds(pl.multiple_of(k * ROWS, ROWS), ROWS)
        to = lax.rem(z + jnp.where(d == 0, 1, NZ - 1), NZ) if not isinstance(d, int) else (z_up, z_dn)[d]
        if s < HOPS - 1:
            dst = rb.at[s + 1, row, cols(b)]
        else:
            base = (1 - to // 8) * PLANE * ROWS
            dst = wall.at[pl.ds(pl.multiple_of(base + k * ROWS, ROWS), ROWS), cols(b)]
        return pltpu.make_async_remote_copy(
            rb.at[s, row, cols(b)], dst, ring_s.at[0], ring_r.at[b, s, k], device_id=dev(to, y, me), device_id_type=MESH
        )

    def ring_wait(b, s, k):
        if s < HOPS - 1:
            dst = rb.at[s + 1, pl.ds(k * ROWS, ROWS), cols(b)]
        else:
            dst = wall.at[pl.ds(pl.multiple_of(far * ROWS + k * ROWS, ROWS), ROWS), cols(b)]
        pltpu.make_async_remote_copy(
            dst, dst, ring_s.at[0], ring_r.at[b, s, k], device_id=up, device_id_type=MESH
        ).wait_recv()

    def bring_copy(s, d):
        rows = pl.ds(d * 16, 16)
        src = lf.at[rows, :] if s == 0 else rbb.at[s - 1, rows, :]
        return pltpu.make_async_remote_copy(
            src, rbb.at[s, rows, :], bring_s.at[s, d], bring_r.at[s, d], device_id=(up, dn)[d], device_id_type=MESH
        )

    def bplane_copy(i, which):
        k = plane[i]
        if which == 0:
            src, q = lf, t
        else:
            src, q = rbb.at[HOPS - 1], far + me
        return pltpu.make_async_remote_copy(
            src,
            ball.at[pl.ds(pl.multiple_of(q * ROWS, ROWS), ROWS), :],
            bp_s.at[which, i],
            bp_r.at[which, me],
            device_id=dev(z, y, k),
            device_id_type=MESH,
        )

    def bplane_wait(k, which):
        q = (t // PLANE) * PLANE + k if which == 0 else far + k
        dst = ball.at[pl.ds(pl.multiple_of(q * ROWS, ROWS), ROWS), :]
        pltpu.make_async_remote_copy(
            dst, dst, bp_s.at[which, 0], bp_r.at[which, k], device_id=up, device_id_type=MESH
        ).wait_recv()

    def y_copy(b, i):
        return pltpu.make_async_remote_copy(
            psy[b].at[y], psy[b].at[y], y_s.at[b, i], y_r.at[b, y], device_id=dev(z, y_peers[i], me), device_id_type=MESH
        )

    def y_wait(b, q):
        pltpu.make_async_remote_copy(
            psy[b].at[q], psy[b].at[q], y_s.at[b, 0], y_r.at[b, q], device_id=up, device_id_type=MESH
        ).wait_recv()

    def z_copy(b, i):
        return pltpu.make_async_remote_copy(
            psz[b].at[zlo],
            psz[b].at[zlo],
            z_s.at[b, i],
            z_r.at[b, zlo],
            device_id=dev(half * 8 + z_peers[i], y, me),
            device_id_type=MESH,
        )

    def z_wait(b, q):
        pltpu.make_async_remote_copy(
            psz[b].at[q], psz[b].at[q], z_s.at[b, 0], z_r.at[b, q], device_id=up, device_id_type=MESH
        ).wait_recv()

    def squares(b, j):
        c = slice((C0[b] + j) * BLOCK, (C0[b] + j + 1) * BLOCK)
        total = jnp.zeros((1, BLOCK), jnp.float32)
        for i in range(4):
            r = slice(i * BLOCK, (i + 1) * BLOCK)
            v = wall[r, c].astype(jnp.float32) + jnp.dot(
                ball[r, :], rfv[:, c], preferred_element_type=jnp.float32
            )
            comb[r, c] = v
            total = total + jnp.sum(v * v, axis=0, keepdims=True)
        psy[b][pl.ds(y, 1), j : j + 1, :] = total[None]

    def finish(b, j):
        g = C0[b] + j
        c = slice(g * BLOCK, (g + 1) * BLOCK)
        total = jnp.sum(psz[b][:, j, :], axis=0, keepdims=True)
        factor = magv[pl.ds(t * 13 + g, 1), :] / jnp.sqrt(total + EPS)
        rid = lax.broadcasted_iota(jnp.int32, (8, BLOCK), 0)
        cid = lax.broadcasted_iota(jnp.int32, (8, BLOCK), 1)
        for i in range(4):
            r = slice(i * BLOCK, (i + 1) * BLOCK)
            m = (comb[r, c] * factor).astype(jnp.bfloat16).astype(jnp.float32)
            top = jnp.max(jnp.max(jnp.abs(m), axis=0, keepdims=True), axis=1, keepdims=True)
            outv[r, c] = (m * (1.0 / (top + EPS))).astype(jnp.bfloat16)
            scv[...] = jnp.where((rid == i) & (cid == g), top, scv[...])

    def out_copy(b):
        return pltpu.make_async_copy(outv.at[:, cols(b)], out.at[:, cols(b)], outs.at[b])

    def pieces(b):
        def arrive():
            for k in range(PLANE):
                ring_wait(b, HOPS - 1, k)
            if b == 0:
                for k in plane:
                    own_wait(k)
                    bplane_wait(k, 0)
                    bplane_wait(k, 1)
                for c in loads:
                    c.wait()

        def y_send():
            for i in range(3):
                y_copy(b, i).start()

        def y_sum():
            for q in y_peers:
                y_wait(b, q)
            psz[b][pl.ds(zlo, 1)] = jnp.sum(psy[b][...], axis=0, keepdims=True)
            for i in range(7):
                z_copy(b, i).start()

        def z_sum():
            for q in z_peers:
                z_wait(b, q)

        todo = [(6, arrive)]
        todo += [(7 + j, functools.partial(squares, b, j)) for j in range(NB[b])]
        todo += [(7 + NB[b], y_send), (12 + NB[b], y_sum), (22 + NB[b], z_sum)]
        todo += [(23 + NB[b] + j, functools.partial(finish, b, j)) for j in range(NB[b])]
        todo += [(23 + 2 * NB[b], lambda: out_copy(b).start())]
        return todo

    for d in range(2):
        bring_copy(0, d).start()
    for i in range(7):
        stage_copy(0, i).start()
    for i in range(7):
        bplane_copy(i, 0).start()
    for i in range(7):
        own_copy(i).start()
    for b in range(1, len(NB)):
        for i in range(7):
            stage_copy(b, i).start()
    scv[...] = jnp.zeros_like(scv)

    queue = []
    for b in range(len(NB)):
        slot = 0
        for s in range(HOPS):
            if b == 0 and s > 0:
                for d in range(2):
                    bring_copy(s - 1, d).wait_recv()
                    bring_copy(s, d).start()
            order = [me] + plane if s == 0 else [0, 4, 1, 5, 2, 6, 3, 7]
            for n, k in enumerate(order):
                if s == 0:
                    if b == 0 and n == 0:
                        own_stage.wait()
                    if n > 0:
                        stage_wait(b, k)
                    ring_copy(b, s, k, jnp.where(k < 4, 0, 1)).start()
                else:
                    ring_wait(b, s - 1, k)
                    ring_copy(b, s, k, k // 4).start()
                if n % 2 == 1:
                    while queue and queue[0][0] <= slot:
                        queue.pop(0)[1]()
                        break
                    slot += 1
        if b == 0:
            for d in range(2):
                bring_copy(HOPS - 1, d).wait_recv()
            fill = pltpu.make_async_copy(
                rbb.at[HOPS - 1], ball.at[pl.ds(pl.multiple_of((far + me) * ROWS, ROWS), ROWS), :], loc.at[5]
            )
            fill.start()
            loads.append(fill)
            for i in range(7):
                bplane_copy(i, 1).start()
        while queue:
            queue.pop(0)[1]()
        queue = pieces(b)
    while queue:
        queue.pop(0)[1]()

    pltpu.make_async_remote_copy(rb, rb, ring_s.at[0], ring_r.at[0, 0, 0], device_id=up, device_id_type=MESH).wait_send()
    both = wall.at[pl.ds(0, 14 * ROWS), :]
    pltpu.make_async_remote_copy(both, both, pl_s.at[0], own_r.at[0], device_id=up, device_id_type=MESH).wait_send()
    for s in range(HOPS):
        for d in range(2):
            bring_copy(s, d).wait_send()
    for i in range(7):
        for which in range(2):
            bplane_copy(i, which).wait_send()
    for b in range(len(NB)):
        for i in range(3):
            y_copy(b, i).wait_send()
        for i in range(7):
            z_copy(b, i).wait_send()
    scales[...] = scv[0:4, 0:13]
    for b in range(len(NB)):
        out_copy(b).wait()


def body(base_weight, left_factor, right_factor, magnitude):
    bf, f32 = jnp.bfloat16, jnp.float32
    dma = pltpu.SemaphoreType.DMA
    nb = len(NB)
    anywhere = pl.BlockSpec(memory_space=pl.ANY)
    return pl.pallas_call(
        kernel,
        name="merge",
        out_shape=(
            jax.ShapeDtypeStruct((16 * ROWS, COLS), bf),
            jax.ShapeDtypeStruct((4, 13), f32),
        ),
        in_specs=[anywhere] * 4,
        out_specs=(anywhere, pl.BlockSpec(memory_space=pltpu.VMEM)),
        scratch_shapes=[
            pltpu.VMEM((16 * ROWS, COLS), bf),
            pltpu.VMEM((HOPS, PLANE * ROWS, COLS), bf),
            pltpu.VMEM((16 * ROWS, 64), bf),
            pltpu.VMEM((HOPS, ROWS, 64), bf),
            pltpu.VMEM((64, COLS), bf),
            pltpu.VMEM((208, BLOCK), f32),
            pltpu.VMEM((16 * ROWS, COLS), f32),
            pltpu.VMEM((16 * ROWS, COLS), bf),
            *[pltpu.VMEM((NY, n, BLOCK), f32) for n in NB],
            *[pltpu.VMEM((8, n, BLOCK), f32) for n in NB],
            pltpu.VMEM((8, BLOCK), f32),
            dma((1,)),
            dma((nb, HOPS, PLANE)),
            dma((HOPS, 2)),
            dma((HOPS, 2)),
            dma((1,)),
            dma((nb, PLANE)),
            dma((PLANE,)),
            dma((2, 7)),
            dma((2, PLANE)),
            dma((nb, 3)),
            dma((nb, NY)),
            dma((nb, 7)),
            dma((nb, 8)),
            dma((6,)),
            dma((nb,)),
        ],
        compiler_params=pltpu.CompilerParams(collective_id=0, has_side_effects=True),
    )(base_weight, left_factor, right_factor, magnitude.reshape(208, BLOCK))


def solution(mesh):
    in_specs = (P(("fsdp", "tp"), None), P(("fsdp", "tp"), None), P(None, "tp"), P())
    out_specs = (P("fsdp", "tp"), P("fsdp", "tp"))
    return jax.shard_map(body, mesh=mesh, in_specs=in_specs, out_specs=out_specs, check_vma=False)
```

```python
import functools

import jax
import jax.numpy as jnp
from jax import lax
from jax.experimental import pallas as pl
from jax.experimental.pallas import tpu as pltpu
from jax.sharding import PartitionSpec as P

MESH = pl.DeviceIdType.MESH
BLOCK = 128
EPS = 1e-06
NB = (5, 4, 4)
C0 = (0, 5, 9)
ROWS = 32
COLS = 1664
CHUNKS = 13
NX = 4
NY = 4
NZ = 16
HOPS = 8
PLANE = 8
UPC = 7 * BLOCK
READY = {0: 1.0, 1: 8.0, 3: 8.0, 2: 17.0}
DXS = (0, 1, 3, 2)


def ring_order():
    at = {(dx, r): [0, READY[dx]] for dx in DXS for r in range(len(NB))}
    now, order = 0.0, []
    while any(v[0] < HOPS - 1 for v in at.values()):
        ready = [(v[0], r, DXS.index(dx), dx) for (dx, r), v in at.items() if v[0] < HOPS - 1 and v[1] <= now]
        if not ready:
            now += 0.1
            continue
        s, r, _, dx = min(ready)
        order.append((now, s, dx, r))
        now += 0.18 * NB[r]
        at[dx, r] = [s + 1, now + 2.2]
    for r in range(len(NB)):
        for xs in range(NX):
            order.append((now, HOPS - 1, xs, r))
            now += 0.18 * NB[r]
    return order


def kernel(
    w, lf, rf, mag, out, scales, wall, rb, ball, rbb, rfv, apv, magv, facv, comb, outv, ps, ry, pay, zs, tz, scv,
    ring_s, ring_r, bring_s, bring_r, pl_s, st_r, own_r, bp_s, bp_r, ap_s, ap_r, ay_s, ay_r, y_s, y_r, z_s, z_r,
    g_s, g_r, loc, outs,
):
    f, t = lax.axis_index("fsdp"), lax.axis_index("tp")
    zlo, y = f // NY, lax.rem(f, NY)
    half, x, core = t // PLANE, lax.rem(t, PLANE) // 2, lax.rem(t, 2)
    z = half * 8 + zlo
    me = x * 2 + core
    far = (1 - half) * PLANE

    def dev(zz, yy, k):
        return (lax.rem(zz, 8) * NY + yy, (zz // 8) * PLANE + k)

    z_up, z_dn = lax.rem(z + 1, NZ), lax.rem(z + NZ - 1, NZ)
    up, dn = dev(z_up, y, me), dev(z_dn, y, me)
    plane = [lax.rem(x + dx, NX) * 2 + lax.rem(core + dc, 2) for dx in DXS for dc in (0, 1)][1:]
    y_peers = [lax.rem(y + d, NY) for d in range(1, NY)]
    z_peers = [lax.rem(z + d, NZ) for d in range(1, NZ)]

    def rows(k, n=ROWS):
        return pl.ds(pl.multiple_of(k * n, n), n)

    def cols(r):
        return pl.ds(C0[r] * BLOCK, NB[r] * BLOCK)

    def remote(src, dst, send, recv, to):
        return pltpu.make_async_remote_copy(src, dst, send, recv, device_id=to, device_id_type=MESH)

    own_stage = pltpu.make_async_copy(
        w.at[:, pl.ds(pl.multiple_of((far + me) * COLS, BLOCK), COLS)], rb.at[0, rows(me), :], loc.at[4]
    )
    loads = [
        pltpu.make_async_copy(rf, rfv, loc.at[0]),
        pltpu.make_async_copy(mag, magv, loc.at[1]),
        pltpu.make_async_copy(lf, ball.at[rows(t), :], loc.at[2]),
        pltpu.make_async_copy(w.at[:, pl.ds(pl.multiple_of(t * COLS, BLOCK), COLS)], wall.at[rows(t), :], loc.at[3]),
    ]
    own_stage.start()
    for c in loads:
        c.start()

    barrier = pltpu.get_barrier_semaphore()
    peers = [up, dn] + [dev(z, y, k) for k in plane] + [dev(z, q, me) for q in y_peers]
    for p in peers:
        pl.semaphore_signal(barrier, inc=1, device_id=p, device_id_type=MESH)
    pl.semaphore_wait(barrier, len(peers))

    def stage_copy(i):
        k = plane[i]
        src = w.at[:, pl.ds(pl.multiple_of((far + k) * COLS, BLOCK), COLS)]
        return remote(src, rb.at[0, rows(me), :], pl_s.at[0], st_r.at[me], dev(z, y, k))

    def stage_wait(k):
        remote(rb.at[0, rows(k), :], rb.at[0, rows(k), :], pl_s.at[0], st_r.at[k], up).wait_recv()

    def own_copy(i):
        k = plane[i]
        src = w.at[:, pl.ds(pl.multiple_of((half * PLANE + k) * COLS, BLOCK), COLS)]
        return remote(src, wall.at[rows(t), :], pl_s.at[0], own_r.at[me], dev(z, y, k))

    def own_wait(k):
        row = rows(half * PLANE + k)
        remote(wall.at[row, :], wall.at[row, :], pl_s.at[0], own_r.at[k], up).wait_recv()

    def ring_copy(r, s, k, d):
        to = (z_up, z_dn)[d] if isinstance(d, int) else lax.rem(z + jnp.where(d == 0, 1, NZ - 1), NZ)
        if s < HOPS - 1:
            dst = rb.at[s + 1, rows(k), cols(r)]
        else:
            dst = wall.at[rows((1 - to // 8) * PLANE + k), cols(r)]
        return remote(rb.at[s, rows(k), cols(r)], dst, ring_s.at[0], ring_r.at[r, s, k], dev(to, y, me))

    def ring_wait(r, s, k):
        dst = rb.at[s + 1, rows(k), cols(r)] if s < HOPS - 1 else wall.at[rows(far + k), cols(r)]
        remote(dst, dst, ring_s.at[0], ring_r.at[r, s, k], up).wait_recv()

    def bring_copy(s, d):
        part = pl.ds(d * 16, 16)
        src = lf.at[part, :] if s == 0 else rbb.at[s - 1, part, :]
        return remote(src, rbb.at[s, part, :], bring_s.at[s, d], bring_r.at[s, d], (up, dn)[d])

    def bplane_copy(i, which):
        src, q = (lf, t) if which == 0 else (rbb.at[HOPS - 1], far + me)
        return remote(src, ball.at[rows(q), :], bp_s.at[which, i], bp_r.at[which, me], dev(z, y, plane[i]))

    def bplane_wait(k, which):
        dst = ball.at[rows((half * PLANE if which == 0 else far) + k), :]
        remote(dst, dst, bp_s.at[which, 0], bp_r.at[which, k], up).wait_recv()

    def chain(d, own):
        c = (pl.ds(0, UPC), pl.ds(UPC, COLS - UPC))[d]
        dst = apv.at[rows(y, 16), c]
        return remote(rf.at[rows(y, 16), c] if own else dst, dst, ap_s.at[d], ap_r.at[d], (up, dn)[d])

    def chain_step(j):
        for d in range(2):
            place = zlo if d == 0 else 7 - zlo
            if j == 0:
                pl.when(place == 7)(lambda: chain(d, True).start())
            else:

                @pl.when(place == j - 1)
                def _():
                    chain(d, False).wait_recv()
                    if j < 8:
                        chain(d, False).start()

    def share_copy(i):
        part = apv.at[rows(y, 16), :]
        return remote(part, part, ay_s.at[i], ay_r.at[y], dev(z, y_peers[i], me))

    def share_wait(q):
        part = apv.at[rows(q, 16), :]
        remote(part, part, ay_s.at[0], ay_r.at[q], up).wait_recv()

    def hop_step(j):
        for d in range(2):
            if j > 0:
                bring_copy(j - 1, d).wait_recv()
            if j < HOPS:
                bring_copy(j, d).start()
        chain_step(j)

    def spread():
        fill = pltpu.make_async_copy(rbb.at[HOPS - 1], ball.at[rows(far + me), :], loc.at[5])
        fill.start()
        loads.append(fill)
        for i in range(7):
            bplane_copy(i, 1).start()
        for i in range(3):
            share_copy(i).start()

    def y_copy(i):
        q = y_peers[i]
        return remote(ps.at[q], ry.at[y], y_s.at[i], y_r.at[y], dev(z, q, me))

    def y_wait(q):
        remote(ry.at[q], ry.at[q], y_s.at[0], y_r.at[q], up).wait_recv()

    def z_copy(i):
        q = z_peers[i]
        src = pay.at[jnp.where(q // 8 == half, 0, 1)]
        return remote(src, zs.at[z], z_s.at[i], z_r.at[z], dev(q, y, me))

    def z_wait(q):
        remote(zs.at[q], zs.at[q], z_s.at[0], z_r.at[q], up).wait_recv()

    def g_copy(i):
        return remote(tz.at[y], tz.at[y], g_s.at[i], g_r.at[y], dev(z, y_peers[i], me))

    def g_wait(q):
        remote(tz.at[q], tz.at[q], g_s.at[0], g_r.at[q], up).wait_recv()

    def arrive():
        for k in plane:
            own_wait(k)
            bplane_wait(k, 0)
        for c in loads[:4]:
            c.wait()
        for q in y_peers:
            share_wait(q)

    mine = rows(half, 256)

    def squares(g):
        c = slice(g * BLOCK, (g + 1) * BLOCK)
        left = ball[mine, :]
        v = wall[mine, c].astype(jnp.float32) + jnp.dot(left, rfv[:, c], preferred_element_type=jnp.float32)
        comb[:, c] = v
        ps[g // 4, 0, g % 4 : g % 4 + 1, :] = jnp.sum(v * v, axis=0, keepdims=True)
        u = rb[0, :, c].astype(jnp.float32) + jnp.dot(left, apv[:, c], preferred_element_type=jnp.float32)
        ps[g // 4, 1, g % 4 : g % 4 + 1, :] = jnp.sum(u * u, axis=0, keepdims=True)

    def y_send():
        for i in range(3):
            y_copy(i).start()
        ry[pl.ds(y, 1)] = ps[pl.ds(y, 1)]

    def z_send():
        for q in y_peers:
            y_wait(q)
        pay[...] = jnp.sum(ry[...], axis=0)
        zs[pl.ds(z, 1)] = pay[0:1]
        for i in range(15):
            z_copy(i).start()

    def g_send():
        for q in z_peers:
            z_wait(q)
        tz[pl.ds(y, 1)] = jnp.sum(zs[...], axis=0, keepdims=True)
        for i in range(3):
            g_copy(i).start()

    def factors():
        for q in y_peers:
            g_wait(q)
        for g in range(CHUNKS):
            total = tz[g // 4, g % 4 : g % 4 + 1, :]
            facv[g : g + 1, :] = magv[pl.ds(t * CHUNKS + g, 1), :] / jnp.sqrt(total + EPS)

    rid = lax.broadcasted_iota(jnp.int32, (8, BLOCK), 0)
    cid = lax.broadcasted_iota(jnp.int32, (8, BLOCK), 1)

    def quantize(v, g, block_row):
        m = (v * facv[g : g + 1, :]).astype(jnp.bfloat16).astype(jnp.float32)
        top = jnp.max(jnp.max(jnp.abs(m), axis=0, keepdims=True), axis=1, keepdims=True)
        outv[rows(block_row, BLOCK), g * BLOCK : (g + 1) * BLOCK] = (m * (1.0 / (top + EPS))).astype(jnp.bfloat16)
        scv[...] = jnp.where((rid == block_row) & (cid == g), top, scv[...])

    def finish_own(g):
        for i in range(2):
            quantize(comb[i * BLOCK : (i + 1) * BLOCK, g * BLOCK : (g + 1) * BLOCK], g, half * 2 + i)

    def finish_far(g, i):
        c = slice(g * BLOCK, (g + 1) * BLOCK)
        row = rows((1 - half) * 2 + i, BLOCK)
        v = wall[row, c].astype(jnp.float32) + jnp.dot(ball[row, :], rfv[:, c], preferred_element_type=jnp.float32)
        quantize(v, g, (1 - half) * 2 + i)

    def own_out():
        return pltpu.make_async_copy(outv.at[mine, :], out.at[mine, :], outs.at[0])

    def far_out(r, i):
        row = rows((1 - half) * 2 + i, BLOCK)
        return pltpu.make_async_copy(outv.at[row, cols(r)], out.at[row, cols(r)], outs.at[1 + r * 2 + i])

    def ready_far():
        loads[4].wait()
        for k in plane:
            bplane_wait(k, 1)

    todo = [(1.5 + 3.0 * j, functools.partial(hop_step, j)) for j in range(9)]
    todo += [(26.0, spread), (30.0, arrive)]
    todo += [(30.5 + 0.7 * g, functools.partial(squares, g)) for g in range(CHUNKS)]
    todo += [(40.0, y_send), (44.0, z_send), (54.0, g_send), (57.5, factors)]
    todo += [(58.0, ready_far)]
    todo += [(58.0 + 0.6 * g, functools.partial(finish_own, g)) for g in range(CHUNKS)]
    todo += [(66.0, lambda: own_out().start())]

    own_stage.wait()
    for r in range(len(NB)):
        ring_copy(r, 0, me, core).start()
    for i in range(7):
        stage_copy(i).start()
    for i in range(7):
        bplane_copy(i, 0).start()
    for i in range(7):
        own_copy(i).start()
    ps[...] = jnp.zeros_like(ps)
    scv[...] = jnp.zeros_like(scv)

    staged = set()
    for now, s, dx, r in ring_order():
        if todo and todo[0][0] <= now:
            todo.pop(0)[1]()
        if s == 0 and dx == 0:
            k = x * 2 + 1 - core
            if dx not in staged:
                stage_wait(k)
                staged.add(dx)
            ring_copy(r, 0, k, 1 - core).start()
            continue
        for d in range(2):
            k = (dx if s == HOPS - 1 else lax.rem(x + dx, NX)) * 2 + d
            if s == 0:
                if dx not in staged:
                    stage_wait(k)
            else:
                ring_wait(r, s - 1, k)
            ring_copy(r, s, k, d).start()
        if s == 0:
            staged.add(dx)
    for _, task in todo:
        task()

    for r in range(len(NB)):
        for i in range(2):
            for k in range(4 * i, 4 * i + 4):
                ring_wait(r, HOPS - 1, k)
            for j in range(NB[r]):
                finish_far(C0[r] + j, i)
            far_out(r, i).start()

    scales[...] = scv[0:4, 0:CHUNKS]
    remote(rb, rb, ring_s.at[0], ring_r.at[0, 0, 0], up).wait_send()
    both = wall.at[pl.ds(0, 14 * ROWS), :]
    remote(both, both, pl_s.at[0], own_r.at[0], up).wait_send()
    for s in range(HOPS):
        for d in range(2):
            bring_copy(s, d).wait_send()
    for i in range(7):
        for which in range(2):
            bplane_copy(i, which).wait_send()
    for d in range(2):
        chain(d, False).wait_send()
    for i in range(3):
        share_copy(i).wait_send()
        y_copy(i).wait_send()
        g_copy(i).wait_send()
    for i in range(15):
        z_copy(i).wait_send()
    own_out().wait()
    for r in range(len(NB)):
        for i in range(2):
            far_out(r, i).wait()


def body(base_weight, left_factor, right_factor, magnitude):
    bf, f32 = jnp.bfloat16, jnp.float32
    dma = pltpu.SemaphoreType.DMA
    nb = len(NB)
    anywhere = pl.BlockSpec(memory_space=pl.ANY)
    return pl.pallas_call(
        kernel,
        name="merge",
        out_shape=(
            jax.ShapeDtypeStruct((16 * ROWS, COLS), bf),
            jax.ShapeDtypeStruct((4, CHUNKS), f32),
        ),
        in_specs=[anywhere] * 4,
        out_specs=(anywhere, pl.BlockSpec(memory_space=pltpu.VMEM)),
        scratch_shapes=[
            pltpu.VMEM((16 * ROWS, COLS), bf),
            pltpu.VMEM((HOPS, PLANE * ROWS, COLS), bf),
            pltpu.VMEM((16 * ROWS, 64), bf),
            pltpu.VMEM((HOPS, ROWS, 64), bf),
            pltpu.VMEM((64, COLS), bf),
            pltpu.VMEM((64, COLS), bf),
            pltpu.VMEM((208, BLOCK), f32),
            pltpu.VMEM((16, BLOCK), f32),
            pltpu.VMEM((8 * ROWS, COLS), f32),
            pltpu.VMEM((16 * ROWS, COLS), bf),
            pltpu.VMEM((NY, 2, 4, BLOCK), f32),
            pltpu.VMEM((NY, 2, 4, BLOCK), f32),
            pltpu.VMEM((2, 4, BLOCK), f32),
            pltpu.VMEM((NZ, 4, BLOCK), f32),
            pltpu.VMEM((NY, 4, BLOCK), f32),
            pltpu.VMEM((8, BLOCK), f32),
            dma((1,)),
            dma((nb, HOPS, PLANE)),
            dma((HOPS, 2)),
            dma((HOPS, 2)),
            dma((1,)),
            dma((PLANE,)),
            dma((PLANE,)),
            dma((2, 7)),
            dma((2, PLANE)),
            dma((2,)),
            dma((2,)),
            dma((3,)),
            dma((NY,)),
            dma((3,)),
            dma((NY,)),
            dma((15,)),
            dma((NZ,)),
            dma((3,)),
            dma((NY,)),
            dma((6,)),
            dma((1 + 2 * nb,)),
        ],
        compiler_params=pltpu.CompilerParams(collective_id=0, has_side_effects=True),
    )(base_weight, left_factor, right_factor, magnitude.reshape(208, BLOCK))


def solution(mesh):
    in_specs = (P(("fsdp", "tp"), None), P(("fsdp", "tp"), None), P(None, "tp"), P())
    out_specs = (P("fsdp", "tp"), P("fsdp", "tp"))
    return jax.shard_map(body, mesh=mesh, in_specs=in_specs, out_specs=out_specs, check_vma=False)
```

```python
import functools

import jax
import jax.numpy as jnp
from jax import lax
from jax.experimental import pallas as pl
from jax.experimental.pallas import tpu as pltpu
from jax.sharding import PartitionSpec as P

MESH = pl.DeviceIdType.MESH
BLOCK = 128
EPS = 1e-06
NB = (5, 4, 4)
C0 = (0, 5, 9)
ROWS = 32
COLS = 1664
CHUNKS = 13
NX = 4
NY = 4
NZ = 16
HOPS = 8
PLANE = 8
UPC = 7 * BLOCK
READY = {0: 1.0, 1: 12.0, 3: 12.0, 2: 36.0}
DXS = (0, 1, 3, 2)


def ring_order():
    at = {(dx, r): [0, READY[dx]] for dx in DXS for r in range(len(NB))}
    now, order = 0.0, []
    while any(v[0] < HOPS - 1 for v in at.values()):
        ready = [(v[0], r, DXS.index(dx), dx) for (dx, r), v in at.items() if v[0] < HOPS - 1 and v[1] <= now]
        if not ready:
            now += 0.1
            continue
        s, r, _, dx = min(ready)
        order.append((now, s, dx, r))
        now += 0.18 * NB[r]
        at[dx, r] = [s + 1, now + 2.2]
    for r in range(len(NB)):
        for xs in range(NX):
            order.append((now, HOPS - 1, xs, r))
            now += 0.18 * NB[r]
    return order


def kernel(
    w, lf, rf, mag, outv, scales, wall, rb, ball, rbb, rfv, apv, magv, facv, comb, ps, ry, pay, zs, tz, scv,
    ring_s, ring_r, bring_s, bring_r, pl_s, st_r, own_r, bp_s, bp_r, ap_s, ap_r, ay_s, ay_r, y_s, y_r, z_s, z_r,
    g_s, g_r, loc,
):
    f, t = lax.axis_index("fsdp"), lax.axis_index("tp")
    zlo, y = f // NY, lax.rem(f, NY)
    half, x, core = t // PLANE, lax.rem(t, PLANE) // 2, lax.rem(t, 2)
    z = half * 8 + zlo
    me = x * 2 + core
    far = (1 - half) * PLANE

    def dev(zz, yy, k):
        return (lax.rem(zz, 8) * NY + yy, (zz // 8) * PLANE + k)

    z_up, z_dn = lax.rem(z + 1, NZ), lax.rem(z + NZ - 1, NZ)
    up, dn = dev(z_up, y, me), dev(z_dn, y, me)
    plane = [lax.rem(x + dx, NX) * 2 + lax.rem(core + dc, 2) for dx in DXS for dc in (0, 1)][1:]
    y_peers = [lax.rem(y + d, NY) for d in range(1, NY)]
    z_peers = [lax.rem(z + d, NZ) for d in range(1, NZ)]

    def rows(k, n=ROWS):
        return pl.ds(pl.multiple_of(k * n, n), n)

    def cols(r):
        return pl.ds(C0[r] * BLOCK, NB[r] * BLOCK)

    def remote(src, dst, send, recv, to):
        return pltpu.make_async_remote_copy(src, dst, send, recv, device_id=to, device_id_type=MESH)

    own_stage = pltpu.make_async_copy(
        w.at[:, pl.ds(pl.multiple_of((far + me) * COLS, BLOCK), COLS)], rb.at[0, rows(me), :], loc.at[4]
    )
    loads = [
        pltpu.make_async_copy(rf, rfv, loc.at[0]),
        pltpu.make_async_copy(mag, magv, loc.at[1]),
        pltpu.make_async_copy(lf, ball.at[rows(t), :], loc.at[2]),
        pltpu.make_async_copy(w.at[:, pl.ds(pl.multiple_of(t * COLS, BLOCK), COLS)], wall.at[rows(t), :], loc.at[3]),
    ]
    own_stage.start()
    for c in loads:
        c.start()

    barrier = pltpu.get_barrier_semaphore()
    peers = [up, dn] + [dev(z, y, k) for k in plane] + [dev(z, q, me) for q in y_peers]
    for p in peers:
        pl.semaphore_signal(barrier, inc=1, device_id=p, device_id_type=MESH)
    pl.semaphore_wait(barrier, len(peers))

    def stage_copy(i):
        k = plane[i]
        src = w.at[:, pl.ds(pl.multiple_of((far + k) * COLS, BLOCK), COLS)]
        return remote(src, rb.at[0, rows(me), :], pl_s.at[0], st_r.at[me], dev(z, y, k))

    def stage_wait(k):
        remote(rb.at[0, rows(k), :], rb.at[0, rows(k), :], pl_s.at[0], st_r.at[k], up).wait_recv()

    def own_copy(i):
        k = plane[i]
        src = w.at[:, pl.ds(pl.multiple_of((half * PLANE + k) * COLS, BLOCK), COLS)]
        return remote(src, wall.at[rows(t), :], pl_s.at[0], own_r.at[me], dev(z, y, k))

    def own_wait(k):
        row = rows(half * PLANE + k)
        remote(wall.at[row, :], wall.at[row, :], pl_s.at[0], own_r.at[k], up).wait_recv()

    def ring_copy(r, s, k, d):
        to = (z_up, z_dn)[d] if isinstance(d, int) else lax.rem(z + jnp.where(d == 0, 1, NZ - 1), NZ)
        if s < HOPS - 1:
            dst = rb.at[s + 1, rows(k), cols(r)]
        else:
            dst = wall.at[rows((1 - to // 8) * PLANE + k), cols(r)]
        return remote(rb.at[s, rows(k), cols(r)], dst, ring_s.at[0], ring_r.at[r, s, k], dev(to, y, me))

    def ring_wait(r, s, k):
        dst = rb.at[s + 1, rows(k), cols(r)] if s < HOPS - 1 else wall.at[rows(far + k), cols(r)]
        remote(dst, dst, ring_s.at[0], ring_r.at[r, s, k], up).wait_recv()

    def bring_copy(s, d):
        part = pl.ds(d * 16, 16)
        src = lf.at[part, :] if s == 0 else rbb.at[s - 1, part, :]
        return remote(src, rbb.at[s, part, :], bring_s.at[s, d], bring_r.at[s, d], (up, dn)[d])

    def bplane_copy(i, which):
        src, q = (lf, t) if which == 0 else (rbb.at[HOPS - 1], far + me)
        return remote(src, ball.at[rows(q), :], bp_s.at[which, i], bp_r.at[which, me], dev(z, y, plane[i]))

    def bplane_wait(k, which):
        dst = ball.at[rows((half * PLANE if which == 0 else far) + k), :]
        remote(dst, dst, bp_s.at[which, 0], bp_r.at[which, k], up).wait_recv()

    def chain(d, own):
        c = (pl.ds(0, UPC), pl.ds(UPC, COLS - UPC))[d]
        dst = apv.at[rows(y, 16), c]
        return remote(rf.at[rows(y, 16), c] if own else dst, dst, ap_s.at[d], ap_r.at[d], (up, dn)[d])

    def chain_step(j):
        for d in range(2):
            place = zlo if d == 0 else 7 - zlo
            if j == 0:
                pl.when(place == 7)(lambda: chain(d, True).start())
            else:

                @pl.when(place == j - 1)
                def _():
                    chain(d, False).wait_recv()
                    if j < 8:
                        chain(d, False).start()

    def share_copy(i):
        part = apv.at[rows(y, 16), :]
        return remote(part, part, ay_s.at[i], ay_r.at[y], dev(z, y_peers[i], me))

    def share_wait(q):
        part = apv.at[rows(q, 16), :]
        remote(part, part, ay_s.at[0], ay_r.at[q], up).wait_recv()

    def hop_step(j):
        for d in range(2):
            if j > 0:
                bring_copy(j - 1, d).wait_recv()
            if j < HOPS:
                bring_copy(j, d).start()
        chain_step(j)

    def spread():
        fill = pltpu.make_async_copy(rbb.at[HOPS - 1], ball.at[rows(far + me), :], loc.at[5])
        fill.start()
        loads.append(fill)
        for i in range(7):
            bplane_copy(i, 1).start()
        for i in range(3):
            share_copy(i).start()

    def y_copy(i):
        q = y_peers[i]
        return remote(ps.at[q], ry.at[y], y_s.at[i], y_r.at[y], dev(z, q, me))

    def y_wait(q):
        remote(ry.at[q], ry.at[q], y_s.at[0], y_r.at[q], up).wait_recv()

    def z_copy(i):
        q = z_peers[i]
        src = pay.at[jnp.where(q // 8 == half, 0, 1)]
        return remote(src, zs.at[z], z_s.at[i], z_r.at[z], dev(q, y, me))

    def z_wait(q):
        remote(zs.at[q], zs.at[q], z_s.at[0], z_r.at[q], up).wait_recv()

    def g_copy(i):
        return remote(tz.at[y], tz.at[y], g_s.at[i], g_r.at[y], dev(z, y_peers[i], me))

    def g_wait(q):
        remote(tz.at[q], tz.at[q], g_s.at[0], g_r.at[q], up).wait_recv()

    staged = set()

    def staged_by(dx):
        if dx not in staged:
            staged.add(dx)
            for d in range(2):
                if dx > 0:
                    stage_wait(lax.rem(x + dx, NX) * 2 + d)
            if dx == 0:
                stage_wait(x * 2 + 1 - core)

    def arrive():
        for dx in DXS:
            staged_by(dx)
        for k in plane:
            own_wait(k)
            bplane_wait(k, 0)
        for c in loads[:4]:
            c.wait()
        for q in y_peers:
            share_wait(q)

    mine = rows(half, 256)

    def squares(g):
        c = slice(g * BLOCK, (g + 1) * BLOCK)
        left = ball[mine, :]
        v = wall[mine, c].astype(jnp.float32) + jnp.dot(left, rfv[:, c], preferred_element_type=jnp.float32)
        comb[:, c] = v
        ps[g // 4, 0, g % 4 : g % 4 + 1, :] = jnp.sum(v * v, axis=0, keepdims=True)
        u = rb[0, :, c].astype(jnp.float32) + jnp.dot(left, apv[:, c], preferred_element_type=jnp.float32)
        ps[g // 4, 1, g % 4 : g % 4 + 1, :] = jnp.sum(u * u, axis=0, keepdims=True)

    def y_send():
        for i in range(3):
            y_copy(i).start()
        ry[pl.ds(y, 1)] = ps[pl.ds(y, 1)]

    def z_send():
        for q in y_peers:
            y_wait(q)
        pay[...] = jnp.sum(ry[...], axis=0)
        zs[pl.ds(z, 1)] = pay[0:1]
        for i in range(15):
            z_copy(i).start()

    def g_send():
        for q in z_peers:
            z_wait(q)
        tz[pl.ds(y, 1)] = jnp.sum(zs[...], axis=0, keepdims=True)
        for i in range(3):
            g_copy(i).start()

    def factors():
        for q in y_peers:
            g_wait(q)
        for g in range(CHUNKS):
            total = tz[g // 4, g % 4 : g % 4 + 1, :]
            facv[g : g + 1, :] = magv[pl.ds(t * CHUNKS + g, 1), :] / jnp.sqrt(total + EPS)

    rid = lax.broadcasted_iota(jnp.int32, (8, BLOCK), 0)
    cid = lax.broadcasted_iota(jnp.int32, (8, BLOCK), 1)

    def quantize(v, g, block_row):
        m = (v * facv[g : g + 1, :]).astype(jnp.bfloat16).astype(jnp.float32)
        top = jnp.max(jnp.max(jnp.abs(m), axis=0, keepdims=True), axis=1, keepdims=True)
        outv[rows(block_row, BLOCK), g * BLOCK : (g + 1) * BLOCK] = (m * (1.0 / (top + EPS))).astype(jnp.bfloat16)
        scv[...] = jnp.where((rid == block_row) & (cid == g), top, scv[...])

    def finish_own(g):
        for i in range(2):
            quantize(comb[i * BLOCK : (i + 1) * BLOCK, g * BLOCK : (g + 1) * BLOCK], g, half * 2 + i)

    def finish_far(g, i):
        c = slice(g * BLOCK, (g + 1) * BLOCK)
        row = rows((1 - half) * 2 + i, BLOCK)
        v = wall[row, c].astype(jnp.float32) + jnp.dot(ball[row, :], rfv[:, c], preferred_element_type=jnp.float32)
        quantize(v, g, (1 - half) * 2 + i)

    def ready_far():
        loads[4].wait()
        for k in plane:
            bplane_wait(k, 1)

    todo = [(1.5 + 3.0 * j, functools.partial(hop_step, j)) for j in range(9)]
    todo += [(26.0, spread), (30.0, arrive)]
    todo += [(30.5 + 0.7 * g, functools.partial(squares, g)) for g in range(CHUNKS)]
    todo += [(40.0, y_send), (44.0, z_send), (56.0, g_send), (59.5, factors)]
    todo += [(60.0, ready_far)]
    todo += [(60.0 + 0.6 * g, functools.partial(finish_own, g)) for g in range(CHUNKS)]

    own_stage.wait()
    for r in range(len(NB)):
        ring_copy(r, 0, me, core).start()
    for i in range(7):
        stage_copy(i).start()
    for i in range(7):
        bplane_copy(i, 0).start()
    for i in range(7):
        own_copy(i).start()
    ps[...] = jnp.zeros_like(ps)
    scv[...] = jnp.zeros_like(scv)

    for now, s, dx, r in ring_order():
        if todo and todo[0][0] <= now:
            todo.pop(0)[1]()
        if s == 0:
            staged_by(dx)
        if s == 0 and dx == 0:
            ring_copy(r, 0, x * 2 + 1 - core, 1 - core).start()
            continue
        for d in range(2):
            k = (dx if s == HOPS - 1 else lax.rem(x + dx, NX)) * 2 + d
            if s > 0:
                ring_wait(r, s - 1, k)
            ring_copy(r, s, k, d).start()
    for _, task in todo:
        task()

    for r in range(len(NB)):
        for i in range(2):
            for k in range(4 * i, 4 * i + 4):
                ring_wait(r, HOPS - 1, k)
            for j in range(NB[r]):
                finish_far(C0[r] + j, i)

    scales[...] = scv[0:4, 0:CHUNKS]
    remote(rb, rb, ring_s.at[0], ring_r.at[0, 0, 0], up).wait_send()
    both = wall.at[pl.ds(0, 14 * ROWS), :]
    remote(both, both, pl_s.at[0], own_r.at[0], up).wait_send()
    for s in range(HOPS):
        for d in range(2):
            bring_copy(s, d).wait_send()
    for i in range(7):
        for which in range(2):
            bplane_copy(i, which).wait_send()
    for d in range(2):
        chain(d, False).wait_send()
    for i in range(3):
        share_copy(i).wait_send()
        y_copy(i).wait_send()
        g_copy(i).wait_send()
    for i in range(15):
        z_copy(i).wait_send()


def body(base_weight, left_factor, right_factor, magnitude):
    bf, f32 = jnp.bfloat16, jnp.float32
    dma = pltpu.SemaphoreType.DMA
    nb = len(NB)
    anywhere = pl.BlockSpec(memory_space=pl.ANY)
    return pl.pallas_call(
        kernel,
        name="merge",
        out_shape=(
            pltpu.VMEM((16 * ROWS, COLS), bf),
            pltpu.VMEM((4, CHUNKS), f32),
        ),
        in_specs=[anywhere] * 4,
        out_specs=(pl.BlockSpec(memory_space=pltpu.VMEM),) * 2,
        scratch_shapes=[
            pltpu.VMEM((16 * ROWS, COLS), bf),
            pltpu.VMEM((HOPS, PLANE * ROWS, COLS), bf),
            pltpu.VMEM((16 * ROWS, 64), bf),
            pltpu.VMEM((HOPS, ROWS, 64), bf),
            pltpu.VMEM((64, COLS), bf),
            pltpu.VMEM((64, COLS), bf),
            pltpu.VMEM((208, BLOCK), f32),
            pltpu.VMEM((16, BLOCK), f32),
            pltpu.VMEM((8 * ROWS, COLS), f32),
            pltpu.VMEM((NY, 2, 4, BLOCK), f32),
            pltpu.VMEM((NY, 2, 4, BLOCK), f32),
            pltpu.VMEM((2, 4, BLOCK), f32),
            pltpu.VMEM((NZ, 4, BLOCK), f32),
            pltpu.VMEM((NY, 4, BLOCK), f32),
            pltpu.VMEM((8, BLOCK), f32),
            dma((1,)),
            dma((nb, HOPS, PLANE)),
            dma((HOPS, 2)),
            dma((HOPS, 2)),
            dma((1,)),
            dma((PLANE,)),
            dma((PLANE,)),
            dma((2, 7)),
            dma((2, PLANE)),
            dma((2,)),
            dma((2,)),
            dma((3,)),
            dma((NY,)),
            dma((3,)),
            dma((NY,)),
            dma((15,)),
            dma((NZ,)),
            dma((3,)),
            dma((NY,)),
            dma((6,)),
        ],
        compiler_params=pltpu.CompilerParams(collective_id=0, has_side_effects=True),
    )(base_weight, left_factor, right_factor, magnitude.reshape(208, BLOCK))


def solution(mesh):
    in_specs = (P(("fsdp", "tp"), None), P(("fsdp", "tp"), None), P(None, "tp"), P())
    out_specs = (P("fsdp", "tp"), P("fsdp", "tp"))
    return jax.shard_map(body, mesh=mesh, in_specs=in_specs, out_specs=out_specs, check_vma=False)
```

```python
import functools

import jax
import jax.numpy as jnp
from jax import lax
from jax.experimental import pallas as pl
from jax.experimental.pallas import tpu as pltpu
from jax.sharding import PartitionSpec as P

MESH = pl.DeviceIdType.MESH
BLOCK = 128
EPS = 1e-06
NB = (3, 7, 3)
C0 = (0, 3, 10)
ROWS = 32
COLS = 1664
CHUNKS = 13
NX = 4
NY = 4
NZ = 16
HOPS = 8
PLANE = 8
UPC = 7 * BLOCK
READY = {0: 1.0, 1: 12.0, 3: 12.0, 2: 26.0}
DXS = (0, 1, 3, 2)


def ring_order():
    at = {(dx, r): [0, READY[dx] if r else 0.0] for dx in DXS for r in range(len(NB))}

    def more(r, s):
        return s < HOPS - (1 if r else 0)

    now, order = 0.0, []
    while any(more(r, v[0]) for (_, r), v in at.items()):
        ready = [(min(r, 1), v[0], r, DXS.index(dx), dx) for (dx, r), v in at.items() if more(r, v[0]) and v[1] <= now]
        if not ready:
            now += 0.1
            continue
        _, s, r, _, dx = min(ready)
        order.append((now, s, dx, r))
        now += 0.18 * NB[r]
        at[dx, r] = [s + 1, now + 2.2]
    for r in range(1, len(NB)):
        for xs in range(NX):
            order.append((now, HOPS - 1, xs, r))
            now += 0.18 * NB[r]
    return order


def kernel(
    w, lf, rf, mag, outv, scales, wall, rb, ball, rbb, rfv, apv, magv, facv, comb, ps, ry, pay, zs, tz, scv,
    ring_s, ring_r, bring_s, bring_r, pl_s, st_r, own_r, bp_s, bp_r, ap_s, ap_r, ay_s, ay_r, y_s, y_r, z_s, z_r,
    g_s, g_r, sc_s, sc_r, loc,
):
    f, t = lax.axis_index("fsdp"), lax.axis_index("tp")
    zlo, y = f // NY, lax.rem(f, NY)
    half, x, core = t // PLANE, lax.rem(t, PLANE) // 2, lax.rem(t, 2)
    z = half * 8 + zlo
    me = x * 2 + core
    far = (1 - half) * PLANE

    def dev(zz, yy, k):
        return (lax.rem(zz, 8) * NY + yy, (zz // 8) * PLANE + k)

    z_up, z_dn = lax.rem(z + 1, NZ), lax.rem(z + NZ - 1, NZ)
    up, dn = dev(z_up, y, me), dev(z_dn, y, me)
    plane = [lax.rem(x + dx, NX) * 2 + lax.rem(core + dc, 2) for dx in DXS for dc in (0, 1)][1:]
    y_peers = [lax.rem(y + d, NY) for d in range(1, NY)]
    z_peers = [lax.rem(z + d, NZ) for d in range(1, NZ)]

    def rows(k, n=ROWS):
        return pl.ds(pl.multiple_of(k * n, n), n)

    rest = pl.ds(C0[1] * BLOCK, COLS - C0[1] * BLOCK)

    def wide(k):
        return pl.ds(pl.multiple_of((far + k) * COLS + C0[1] * BLOCK, BLOCK), COLS - C0[1] * BLOCK)

    def cols(r):
        return pl.ds(C0[r] * BLOCK, NB[r] * BLOCK)

    def remote(src, dst, send, recv, to):
        return pltpu.make_async_remote_copy(src, dst, send, recv, device_id=to, device_id_type=MESH)

    own_stage = pltpu.make_async_copy(
        w.at[:, wide(me)], rb.at[0, rows(me), rest], loc.at[4]
    )
    loads = [
        pltpu.make_async_copy(rf, rfv, loc.at[0]),
        pltpu.make_async_copy(mag, magv, loc.at[1]),
        pltpu.make_async_copy(lf, ball.at[rows(t), :], loc.at[2]),
        pltpu.make_async_copy(w.at[:, pl.ds(pl.multiple_of(t * COLS, BLOCK), COLS)], wall.at[rows(t), :], loc.at[3]),
    ]
    own_stage.start()
    for c in loads:
        c.start()

    barrier = pltpu.get_barrier_semaphore()
    peers = [up, dn] + [dev(z, y, k) for k in plane] + [dev(z, q, me) for q in y_peers]
    for p in peers:
        pl.semaphore_signal(barrier, inc=1, device_id=p, device_id_type=MESH)
    pl.semaphore_wait(barrier, len(peers))

    def stage_copy(i):
        k = plane[i]
        return remote(w.at[:, wide(k)], rb.at[0, rows(me), rest], pl_s.at[0], st_r.at[me], dev(z, y, k))

    def stage_wait(k):
        remote(rb.at[0, rows(k), rest], rb.at[0, rows(k), rest], pl_s.at[0], st_r.at[k], up).wait_recv()

    def own_copy(i):
        k = plane[i]
        src = w.at[:, pl.ds(pl.multiple_of((half * PLANE + k) * COLS, BLOCK), COLS)]
        return remote(src, wall.at[rows(t), :], pl_s.at[1], own_r.at[me], dev(z, y, k))

    def own_wait(k):
        row = rows(half * PLANE + k)
        remote(wall.at[row, :], wall.at[row, :], pl_s.at[1], own_r.at[k], up).wait_recv()

    def ring_copy(r, s, k, d):
        to = (z_up, z_dn)[d] if isinstance(d, int) else lax.rem(z + jnp.where(d == 0, 1, NZ - 1), NZ)
        if s < HOPS - 1 or r == 0:
            dst = rb.at[(s + 1) % HOPS, rows(k), cols(r)]
        else:
            dst = wall.at[rows((1 - to // 8) * PLANE + k), cols(r)]
        src = rb.at[s, rows(k), cols(r)]
        if s == 0 and r == 0:
            src = w.at[:, pl.ds(pl.multiple_of((far + k) * COLS, BLOCK), NB[0] * BLOCK)]
        return remote(src, dst, ring_s.at[0], ring_r.at[r, s, k], dev(to, y, me))

    def ring_wait(r, s, k):
        if s < HOPS - 1 or r == 0:
            dst = rb.at[(s + 1) % HOPS, rows(k), cols(r)]
        else:
            dst = wall.at[rows(far + k), cols(r)]
        remote(dst, dst, ring_s.at[0], ring_r.at[r, s, k], up).wait_recv()

    def scatter_copy(i):
        src = rb.at[0, rows(plane[i]), cols(0)]
        return remote(src, wall.at[rows(far + me), cols(0)], sc_s.at[i], sc_r.at[me], dev(z, y, plane[i]))

    def scatter_wait(k):
        dst = wall.at[rows(far + k), cols(0)]
        remote(dst, dst, sc_s.at[0], sc_r.at[k], up).wait_recv()

    keep = pltpu.make_async_copy(rb.at[0, rows(me), cols(0)], wall.at[rows(far + me), cols(0)], loc.at[6])

    def scatter():
        for k in range(PLANE):
            ring_wait(0, HOPS - 1, k)
        for i in range(7):
            scatter_copy(i).start()
        keep.start()

    def bring_copy(s, d):
        part = pl.ds(d * 16, 16)
        src = lf.at[part, :] if s == 0 else rbb.at[s - 1, part, :]
        return remote(src, rbb.at[s, part, :], bring_s.at[s, d], bring_r.at[s, d], (up, dn)[d])

    def bplane_copy(i, which):
        src, q = (lf, t) if which == 0 else (rbb.at[HOPS - 1], far + me)
        return remote(src, ball.at[rows(q), :], bp_s.at[which, i], bp_r.at[which, me], dev(z, y, plane[i]))

    def bplane_wait(k, which):
        dst = ball.at[rows((half * PLANE if which == 0 else far) + k), :]
        remote(dst, dst, bp_s.at[which, 0], bp_r.at[which, k], up).wait_recv()

    def chain(d, own):
        c = (pl.ds(0, UPC), pl.ds(UPC, COLS - UPC))[d]
        dst = apv.at[rows(y, 16), c]
        return remote(rf.at[rows(y, 16), c] if own else dst, dst, ap_s.at[d], ap_r.at[d], (up, dn)[d])

    def chain_step(j):
        for d in range(2):
            place = zlo if d == 0 else 7 - zlo
            if j == 0:
                pl.when(place == 7)(lambda: chain(d, True).start())
            else:

                @pl.when(place == j - 1)
                def _():
                    chain(d, False).wait_recv()
                    if j < 8:
                        chain(d, False).start()

    def share_copy(i):
        part = apv.at[rows(y, 16), :]
        return remote(part, part, ay_s.at[i], ay_r.at[y], dev(z, y_peers[i], me))

    def share_wait(q):
        part = apv.at[rows(q, 16), :]
        remote(part, part, ay_s.at[0], ay_r.at[q], up).wait_recv()

    def hop_step(j):
        for d in range(2):
            if j > 0:
                bring_copy(j - 1, d).wait_recv()
            if j < HOPS:
                bring_copy(j, d).start()
        chain_step(j)

    def spread():
        fill = pltpu.make_async_copy(rbb.at[HOPS - 1], ball.at[rows(far + me), :], loc.at[5])
        fill.start()
        loads.append(fill)
        for i in range(7):
            bplane_copy(i, 1).start()
        for i in range(3):
            share_copy(i).start()

    def y_copy(i):
        q = y_peers[i]
        return remote(ps.at[q], ry.at[y], y_s.at[i], y_r.at[y], dev(z, q, me))

    def y_wait(q):
        remote(ry.at[q], ry.at[q], y_s.at[0], y_r.at[q], up).wait_recv()

    def z_copy(i):
        q = z_peers[i]
        src = pay.at[jnp.where(q // 8 == half, 0, 1)]
        return remote(src, zs.at[z], z_s.at[i], z_r.at[z], dev(q, y, me))

    def z_wait(q):
        remote(zs.at[q], zs.at[q], z_s.at[0], z_r.at[q], up).wait_recv()

    def g_copy(i):
        return remote(tz.at[y], tz.at[y], g_s.at[i], g_r.at[y], dev(z, y_peers[i], me))

    def g_wait(q):
        remote(tz.at[q], tz.at[q], g_s.at[0], g_r.at[q], up).wait_recv()

    staged = set()

    def staged_by(dx):
        if dx not in staged:
            staged.add(dx)
            for d in range(2):
                if dx > 0:
                    stage_wait(lax.rem(x + dx, NX) * 2 + d)
            if dx == 0:
                stage_wait(x * 2 + 1 - core)

    def arrive():
        for dx in DXS:
            staged_by(dx)
        for k in plane:
            own_wait(k)
            bplane_wait(k, 0)
        for c in loads[:4]:
            c.wait()
        for q in y_peers:
            share_wait(q)

    mine = rows(half, 256)

    def far_values(g, row):
        c = slice(g * BLOCK, (g + 1) * BLOCK)
        return wall[row, c].astype(jnp.float32) + jnp.dot(ball[row, :], rfv[:, c], preferred_element_type=jnp.float32)

    def squares(g):
        c = slice(g * BLOCK, (g + 1) * BLOCK)
        left = ball[mine, :]
        v = wall[mine, c].astype(jnp.float32) + jnp.dot(left, rfv[:, c], preferred_element_type=jnp.float32)
        comb[:, c] = v
        total = jnp.sum(v * v, axis=0, keepdims=True)
        if g < NB[0]:
            u = far_values(g, rows(1 - half, 256))
            ps[g // 4, 0, g % 4 : g % 4 + 1, :] = total + jnp.sum(u * u, axis=0, keepdims=True)
            return
        ps[g // 4, 0, g % 4 : g % 4 + 1, :] = total
        u = rb[0, :, c].astype(jnp.float32) + jnp.dot(left, apv[:, c], preferred_element_type=jnp.float32)
        ps[g // 4, 1, g % 4 : g % 4 + 1, :] = jnp.sum(u * u, axis=0, keepdims=True)

    def y_send():
        for i in range(3):
            y_copy(i).start()
        ry[pl.ds(y, 1)] = ps[pl.ds(y, 1)]

    def z_send():
        for q in y_peers:
            y_wait(q)
        pay[...] = jnp.sum(ry[...], axis=0)
        zs[pl.ds(z, 1)] = pay[0:1]
        for i in range(15):
            z_copy(i).start()

    def g_send():
        for q in z_peers:
            z_wait(q)
        tz[pl.ds(y, 1)] = jnp.sum(zs[...], axis=0, keepdims=True)
        for i in range(3):
            g_copy(i).start()

    def factors():
        for q in y_peers:
            g_wait(q)
        for g in range(CHUNKS):
            total = tz[g // 4, g % 4 : g % 4 + 1, :]
            facv[g : g + 1, :] = magv[pl.ds(t * CHUNKS + g, 1), :] / jnp.sqrt(total + EPS)

    rid = lax.broadcasted_iota(jnp.int32, (8, BLOCK), 0)
    cid = lax.broadcasted_iota(jnp.int32, (8, BLOCK), 1)

    def quantize(v, g, block_row):
        m = (v * facv[g : g + 1, :]).astype(jnp.bfloat16).astype(jnp.float32)
        top = jnp.max(jnp.max(jnp.abs(m), axis=0, keepdims=True), axis=1, keepdims=True)
        outv[rows(block_row, BLOCK), g * BLOCK : (g + 1) * BLOCK] = (m * (1.0 / (top + EPS))).astype(jnp.bfloat16)
        scv[...] = jnp.where((rid == block_row) & (cid == g), top, scv[...])

    def finish_own(g):
        for i in range(2):
            quantize(comb[i * BLOCK : (i + 1) * BLOCK, g * BLOCK : (g + 1) * BLOCK], g, half * 2 + i)
        far_product(g)

    def finish_far(g, i):
        row = rows((1 - half) * 2 + i, BLOCK)
        c = slice(g * BLOCK, (g + 1) * BLOCK)
        quantize(wall[row, c].astype(jnp.float32) + comb[i * BLOCK : (i + 1) * BLOCK, c], g, (1 - half) * 2 + i)

    def far_product(g):
        c = slice(g * BLOCK, (g + 1) * BLOCK)
        comb[:, c] = jnp.dot(ball[rows(1 - half, 256), :], rfv[:, c], preferred_element_type=jnp.float32)

    def ready_far():
        loads[4].wait()
        for k in plane:
            bplane_wait(k, 1)
            scatter_wait(k)
        keep.wait()

    order = ring_order()
    landed = max(e[0] for e in order if e[3] == 0) + 3.5
    todo = [(2.0 + 3.4 * j, functools.partial(hop_step, j)) for j in range(9)]
    todo += [(30.0, spread), (min(landed, 32.0), scatter), (33.0, arrive)]
    todo += [(33.5 + 0.7 * i, functools.partial(squares, NB[0] + i)) for i in range(CHUNKS - NB[0])]
    todo += [(40.7, ready_far)]
    todo += [(41.0 + 0.7 * i, functools.partial(squares, i)) for i in range(NB[0])]
    todo += [(44.0, y_send), (47.5, z_send), (58.0, g_send), (61.5, factors)]
    todo += [(62.0 + 0.4 * g, functools.partial(finish_own, g)) for g in range(CHUNKS)]
    todo += [(67.5 + 0.4 * g, functools.partial(finish_far, g, i)) for g in range(NB[0]) for i in range(2)]
    todo.sort(key=lambda e: e[0])

    for dx in DXS:
        for d in range(2):
            ring_copy(0, 0, lax.rem(x + dx, NX) * 2 + d, d).start()
    own_stage.wait()
    for r in range(1, len(NB)):
        ring_copy(r, 0, me, core).start()
    for i in range(7):
        stage_copy(i).start()
    for i in range(7):
        bplane_copy(i, 0).start()
    for i in range(7):
        own_copy(i).start()
    ps[...] = jnp.zeros_like(ps)
    scv[...] = jnp.zeros_like(scv)

    for now, s, dx, r in order:
        if todo and todo[0][0] <= now:
            todo.pop(0)[1]()
        if s == 0 and r == 0:
            continue
        if s == 0:
            staged_by(dx)
        if s == 0 and dx == 0:
            ring_copy(r, 0, x * 2 + 1 - core, 1 - core).start()
            continue
        for d in range(2):
            k = (dx if s == HOPS - 1 and r > 0 else lax.rem(x + dx, NX)) * 2 + d
            if s > 0:
                ring_wait(r, s - 1, k)
            ring_copy(r, s, k, d).start()
    for _, task in todo:
        task()

    for r in range(1, len(NB)):
        for i in range(2):
            for k in range(4 * i, 4 * i + 4):
                ring_wait(r, HOPS - 1, k)
            for j in range(NB[r]):
                finish_far(C0[r] + j, i)

    scales[...] = scv[0:4, 0:CHUNKS]
    remote(rb, rb, ring_s.at[0], ring_r.at[0, 0, 0], up).wait_send()
    for n, part in enumerate((wall.at[pl.ds(0, 7 * ROWS), rest], wall.at[pl.ds(0, 7 * ROWS), :])):
        remote(part, part, pl_s.at[n], own_r.at[0], up).wait_send()
    for s in range(HOPS):
        for d in range(2):
            bring_copy(s, d).wait_send()
    for i in range(7):
        scatter_copy(i).wait_send()
        for which in range(2):
            bplane_copy(i, which).wait_send()
    for d in range(2):
        chain(d, False).wait_send()
    for i in range(3):
        share_copy(i).wait_send()
        y_copy(i).wait_send()
        g_copy(i).wait_send()
    for i in range(15):
        z_copy(i).wait_send()


def put(result, scales, out, out_scales, sems):
    copies = [pltpu.make_async_copy(scales, out_scales, sems.at[4])]
    for i in range(4):
        part = pl.ds(i * BLOCK, BLOCK)
        copies.append(pltpu.make_async_copy(result.at[part, :], out.at[part, :], sems.at[i]))
    for c in copies:
        c.start()
    for c in copies:
        c.wait()


def body(base_weight, left_factor, right_factor, magnitude):
    bf, f32 = jnp.bfloat16, jnp.float32
    dma = pltpu.SemaphoreType.DMA
    nb = len(NB)
    anywhere = pl.BlockSpec(memory_space=pl.ANY)
    result, scales = pl.pallas_call(
        kernel,
        name="merge",
        out_shape=(
            pltpu.VMEM((16 * ROWS, COLS), bf),
            pltpu.VMEM((4, CHUNKS), f32),
        ),
        in_specs=[anywhere] * 4,
        out_specs=(pl.BlockSpec(memory_space=pltpu.VMEM),) * 2,
        scratch_shapes=[
            pltpu.VMEM((16 * ROWS, COLS), bf),
            pltpu.VMEM((HOPS, PLANE * ROWS, COLS), bf),
            pltpu.VMEM((16 * ROWS, 64), bf),
            pltpu.VMEM((HOPS, ROWS, 64), bf),
            pltpu.VMEM((64, COLS), bf),
            pltpu.VMEM((64, COLS), bf),
            pltpu.VMEM((208, BLOCK), f32),
            pltpu.VMEM((16, BLOCK), f32),
            pltpu.VMEM((8 * ROWS, COLS), f32),
            pltpu.VMEM((NY, 2, 4, BLOCK), f32),
            pltpu.VMEM((NY, 2, 4, BLOCK), f32),
            pltpu.VMEM((2, 4, BLOCK), f32),
            pltpu.VMEM((NZ, 4, BLOCK), f32),
            pltpu.VMEM((NY, 4, BLOCK), f32),
            pltpu.VMEM((8, BLOCK), f32),
            dma((1,)),
            dma((nb, HOPS, PLANE)),
            dma((HOPS, 2)),
            dma((HOPS, 2)),
            dma((2,)),
            dma((PLANE,)),
            dma((PLANE,)),
            dma((2, 7)),
            dma((2, PLANE)),
            dma((2,)),
            dma((2,)),
            dma((3,)),
            dma((NY,)),
            dma((3,)),
            dma((NY,)),
            dma((15,)),
            dma((NZ,)),
            dma((3,)),
            dma((NY,)),
            dma((7,)),
            dma((PLANE,)),
            dma((7,)),
        ],
        compiler_params=pltpu.CompilerParams(collective_id=0, has_side_effects=True),
    )(base_weight, left_factor, right_factor, magnitude.reshape(208, BLOCK))
    return pl.pallas_call(
        put,
        name="put",
        out_shape=(
            jax.ShapeDtypeStruct((16 * ROWS, COLS), bf),
            jax.ShapeDtypeStruct((4, CHUNKS), f32),
        ),
        in_specs=[pl.BlockSpec(memory_space=pltpu.VMEM)] * 2,
        out_specs=(anywhere, anywhere),
        scratch_shapes=[dma((5,))],
    )(*(pltpu.with_memory_space_constraint(v, pltpu.VMEM) for v in (result, scales)))


def solution(mesh):
    in_specs = (P(("fsdp", "tp"), None), P(("fsdp", "tp"), None), P(None, "tp"), P())
    out_specs = (P("fsdp", "tp"), P("fsdp", "tp"))
    return jax.shard_map(body, mesh=mesh, in_specs=in_specs, out_specs=out_specs, check_vma=False)
```

```python
import functools

import jax
import jax.numpy as jnp
from jax import lax
from jax.experimental import pallas as pl
from jax.experimental.pallas import tpu as pltpu
from jax.sharding import PartitionSpec as P

MESH = pl.DeviceIdType.MESH
BLOCK = 128
EPS = 1e-06
NB = (3, 8, 2)
C0 = (0, 3, 11)
ROWS = 32
COLS = 1664
CHUNKS = 13
NX = 4
NY = 4
NZ = 16
HOPS = 8
PLANE = 8
UPC = 7 * BLOCK
READY = {0: 1.0, 1: 12.0, 3: 12.0, 2: 26.0}
DXS = (0, 1, 3, 2)


def ring_order():
    at = {(dx, r): [0, READY[dx] if r else 0.0] for dx in DXS for r in range(len(NB))}

    def more(r, s):
        return s < HOPS - (1 if r else 0)

    now, order = 0.0, []
    while any(more(r, v[0]) for (_, r), v in at.items()):
        ready = [(min(r, 1), v[0], r, DXS.index(dx), dx) for (dx, r), v in at.items() if more(r, v[0]) and v[1] <= now]
        if not ready:
            now += 0.1
            continue
        _, s, r, _, dx = min(ready)
        order.append((now, s, dx, r))
        now += 0.18 * NB[r]
        at[dx, r] = [s + 1, now + 2.2]
    for r in range(1, len(NB)):
        for xs in range(NX):
            order.append((now, HOPS - 1, xs, r))
            now += 0.18 * NB[r]
    return order


def kernel(
    w, lf, rf, mag, outv, scales, wall, rb, ball, rbb, rfv, apv, magv, facv, comb, ps, ry, pay, zs, tz, scv,
    ring_s, ring_r, bring_s, bring_r, pl_s, st_r, own_r, bp_s, bp_r, ap_s, ap_r, ay_s, ay_r, y_s, y_r, z_s, z_r,
    g_s, g_r, sc_s, sc_r, loc,
):
    f, t = lax.axis_index("fsdp"), lax.axis_index("tp")
    zlo, y = f // NY, lax.rem(f, NY)
    half, x, core = t // PLANE, lax.rem(t, PLANE) // 2, lax.rem(t, 2)
    z = half * 8 + zlo
    me = x * 2 + core
    far = (1 - half) * PLANE

    def dev(zz, yy, k):
        return (lax.rem(zz, 8) * NY + yy, (zz // 8) * PLANE + k)

    z_up, z_dn = lax.rem(z + 1, NZ), lax.rem(z + NZ - 1, NZ)
    up, dn = dev(z_up, y, me), dev(z_dn, y, me)
    plane = [lax.rem(x + dx, NX) * 2 + lax.rem(core + dc, 2) for dx in DXS for dc in (0, 1)][1:]
    y_peers = [lax.rem(y + d, NY) for d in range(1, NY)]
    z_peers = [lax.rem(z + d, NZ) for d in range(1, NZ)]

    def rows(k, n=ROWS):
        return pl.ds(pl.multiple_of(k * n, n), n)

    rest = pl.ds(C0[1] * BLOCK, COLS - C0[1] * BLOCK)

    def wide(k):
        return pl.ds(pl.multiple_of((far + k) * COLS + C0[1] * BLOCK, BLOCK), COLS - C0[1] * BLOCK)

    def cols(r):
        return pl.ds(C0[r] * BLOCK, NB[r] * BLOCK)

    def remote(src, dst, send, recv, to):
        return pltpu.make_async_remote_copy(src, dst, send, recv, device_id=to, device_id_type=MESH)

    own_stage = pltpu.make_async_copy(
        w.at[:, wide(me)], rb.at[0, rows(me), rest], loc.at[4]
    )
    loads = [
        pltpu.make_async_copy(rf, rfv, loc.at[0]),
        pltpu.make_async_copy(mag, magv, loc.at[1]),
        pltpu.make_async_copy(lf, ball.at[rows(t), :], loc.at[2]),
        pltpu.make_async_copy(w.at[:, pl.ds(pl.multiple_of(t * COLS, BLOCK), COLS)], wall.at[rows(t), :], loc.at[3]),
    ]
    own_stage.start()
    for c in loads:
        c.start()

    barrier = pltpu.get_barrier_semaphore()
    peers = [up, dn] + [dev(z, y, k) for k in plane] + [dev(z, q, me) for q in y_peers]
    for p in peers:
        pl.semaphore_signal(barrier, inc=1, device_id=p, device_id_type=MESH)
    pl.semaphore_wait(barrier, len(peers))

    def stage_copy(i):
        k = plane[i]
        return remote(w.at[:, wide(k)], rb.at[0, rows(me), rest], pl_s.at[0], st_r.at[me], dev(z, y, k))

    def stage_wait(k):
        remote(rb.at[0, rows(k), rest], rb.at[0, rows(k), rest], pl_s.at[0], st_r.at[k], up).wait_recv()

    def own_copy(i):
        k = plane[i]
        src = w.at[:, pl.ds(pl.multiple_of((half * PLANE + k) * COLS, BLOCK), COLS)]
        return remote(src, wall.at[rows(t), :], pl_s.at[1], own_r.at[me], dev(z, y, k))

    def own_wait(k):
        row = rows(half * PLANE + k)
        remote(wall.at[row, :], wall.at[row, :], pl_s.at[1], own_r.at[k], up).wait_recv()

    def ring_copy(r, s, k, d):
        to = (z_up, z_dn)[d] if isinstance(d, int) else lax.rem(z + jnp.where(d == 0, 1, NZ - 1), NZ)
        if s < HOPS - 1 or r == 0:
            dst = rb.at[(s + 1) % HOPS, rows(k), cols(r)]
        else:
            dst = wall.at[rows((1 - to // 8) * PLANE + k), cols(r)]
        src = rb.at[s, rows(k), cols(r)]
        if s == 0 and r == 0:
            src = w.at[:, pl.ds(pl.multiple_of((far + k) * COLS, BLOCK), NB[0] * BLOCK)]
        return remote(src, dst, ring_s.at[0], ring_r.at[r, s, k], dev(to, y, me))

    def ring_wait(r, s, k):
        if s < HOPS - 1 or r == 0:
            dst = rb.at[(s + 1) % HOPS, rows(k), cols(r)]
        else:
            dst = wall.at[rows(far + k), cols(r)]
        remote(dst, dst, ring_s.at[0], ring_r.at[r, s, k], up).wait_recv()

    def scatter_copy(i):
        src = rb.at[0, rows(plane[i]), cols(0)]
        return remote(src, wall.at[rows(far + me), cols(0)], sc_s.at[i], sc_r.at[me], dev(z, y, plane[i]))

    def scatter_wait(k):
        dst = wall.at[rows(far + k), cols(0)]
        remote(dst, dst, sc_s.at[0], sc_r.at[k], up).wait_recv()

    keep = pltpu.make_async_copy(rb.at[0, rows(me), cols(0)], wall.at[rows(far + me), cols(0)], loc.at[6])

    def scatter():
        for k in range(PLANE):
            ring_wait(0, HOPS - 1, k)
        for i in range(7):
            scatter_copy(i).start()
        keep.start()

    def bring_copy(s, d):
        part = pl.ds(d * 16, 16)
        src = lf.at[part, :] if s == 0 else rbb.at[s - 1, part, :]
        return remote(src, rbb.at[s, part, :], bring_s.at[s, d], bring_r.at[s, d], (up, dn)[d])

    def bplane_copy(i, which):
        src, q = (lf, t) if which == 0 else (rbb.at[HOPS - 1], far + me)
        return remote(src, ball.at[rows(q), :], bp_s.at[which, i], bp_r.at[which, me], dev(z, y, plane[i]))

    def bplane_wait(k, which):
        dst = ball.at[rows((half * PLANE if which == 0 else far) + k), :]
        remote(dst, dst, bp_s.at[which, 0], bp_r.at[which, k], up).wait_recv()

    def chain(d, own):
        c = (pl.ds(0, UPC), pl.ds(UPC, COLS - UPC))[d]
        dst = apv.at[rows(y, 16), c]
        return remote(rf.at[rows(y, 16), c] if own else dst, dst, ap_s.at[d], ap_r.at[d], (up, dn)[d])

    def chain_step(j):
        for d in range(2):
            place = zlo if d == 0 else 7 - zlo
            if j == 0:
                pl.when(place == 7)(lambda: chain(d, True).start())
            else:

                @pl.when(place == j - 1)
                def _():
                    chain(d, False).wait_recv()
                    if j < 8:
                        chain(d, False).start()

    def share_copy(i):
        part = apv.at[rows(y, 16), :]
        return remote(part, part, ay_s.at[i], ay_r.at[y], dev(z, y_peers[i], me))

    def share_wait(q):
        part = apv.at[rows(q, 16), :]
        remote(part, part, ay_s.at[0], ay_r.at[q], up).wait_recv()

    def hop_step(j):
        for d in range(2):
            if j > 0:
                bring_copy(j - 1, d).wait_recv()
            if j < HOPS:
                bring_copy(j, d).start()
        chain_step(j)

    def spread():
        fill = pltpu.make_async_copy(rbb.at[HOPS - 1], ball.at[rows(far + me), :], loc.at[5])
        fill.start()
        loads.append(fill)
        for i in range(7):
            bplane_copy(i, 1).start()
        for i in range(3):
            share_copy(i).start()

    def y_copy(i):
        q = y_peers[i]
        return remote(ps.at[q], ry.at[y], y_s.at[i], y_r.at[y], dev(z, q, me))

    def y_wait(q):
        remote(ry.at[q], ry.at[q], y_s.at[0], y_r.at[q], up).wait_recv()

    def z_copy(i):
        q = z_peers[i]
        src = pay.at[jnp.where(q // 8 == half, 0, 1)]
        return remote(src, zs.at[z], z_s.at[i], z_r.at[z], dev(q, y, me))

    def z_wait(q):
        remote(zs.at[q], zs.at[q], z_s.at[0], z_r.at[q], up).wait_recv()

    def g_copy(i):
        return remote(tz.at[y], tz.at[y], g_s.at[i], g_r.at[y], dev(z, y_peers[i], me))

    def g_wait(q):
        remote(tz.at[q], tz.at[q], g_s.at[0], g_r.at[q], up).wait_recv()

    staged = set()

    def staged_by(dx):
        if dx not in staged:
            staged.add(dx)
            for d in range(2):
                if dx > 0:
                    stage_wait(lax.rem(x + dx, NX) * 2 + d)
            if dx == 0:
                stage_wait(x * 2 + 1 - core)

    def arrive():
        for dx in DXS:
            staged_by(dx)
        for k in plane:
            own_wait(k)
            bplane_wait(k, 0)
        for c in loads[:4]:
            c.wait()
        for q in y_peers:
            share_wait(q)

    mine = rows(half, 256)

    def far_values(g, row):
        c = slice(g * BLOCK, (g + 1) * BLOCK)
        return wall[row, c].astype(jnp.float32) + jnp.dot(ball[row, :], rfv[:, c], preferred_element_type=jnp.float32)

    def squares(g):
        c = slice(g * BLOCK, (g + 1) * BLOCK)
        left = ball[mine, :]
        v = wall[mine, c].astype(jnp.float32) + jnp.dot(left, rfv[:, c], preferred_element_type=jnp.float32)
        comb[:, c] = v
        total = jnp.sum(v * v, axis=0, keepdims=True)
        if g < NB[0]:
            u = far_values(g, rows(1 - half, 256))
            ps[g // 4, 0, g % 4 : g % 4 + 1, :] = total + jnp.sum(u * u, axis=0, keepdims=True)
            return
        ps[g // 4, 0, g % 4 : g % 4 + 1, :] = total
        u = rb[0, :, c].astype(jnp.float32) + jnp.dot(left, apv[:, c], preferred_element_type=jnp.float32)
        ps[g // 4, 1, g % 4 : g % 4 + 1, :] = jnp.sum(u * u, axis=0, keepdims=True)

    def y_send():
        for i in range(3):
            y_copy(i).start()
        ry[pl.ds(y, 1)] = ps[pl.ds(y, 1)]

    def z_send():
        for q in y_peers:
            y_wait(q)
        pay[...] = jnp.sum(ry[...], axis=0)
        zs[pl.ds(z, 1)] = pay[0:1]
        for i in range(15):
            z_copy(i).start()

    def g_send():
        for q in z_peers:
            z_wait(q)
        tz[pl.ds(y, 1)] = jnp.sum(zs[...], axis=0, keepdims=True)
        for i in range(3):
            g_copy(i).start()

    def factors():
        for q in y_peers:
            g_wait(q)
        for g in range(CHUNKS):
            total = tz[g // 4, g % 4 : g % 4 + 1, :]
            facv[g : g + 1, :] = magv[pl.ds(t * CHUNKS + g, 1), :] / jnp.sqrt(total + EPS)

    rid = lax.broadcasted_iota(jnp.int32, (8, BLOCK), 0)
    cid = lax.broadcasted_iota(jnp.int32, (8, BLOCK), 1)

    def quantize(v, g, block_row):
        m = (v * facv[g : g + 1, :]).astype(jnp.bfloat16).astype(jnp.float32)
        top = jnp.max(jnp.max(jnp.abs(m), axis=0, keepdims=True), axis=1, keepdims=True)
        outv[rows(block_row, BLOCK), g * BLOCK : (g + 1) * BLOCK] = (m * (1.0 / (top + EPS))).astype(jnp.bfloat16)
        scv[...] = jnp.where((rid == block_row) & (cid == g), top, scv[...])

    def finish_own(g):
        for i in range(2):
            quantize(comb[i * BLOCK : (i + 1) * BLOCK, g * BLOCK : (g + 1) * BLOCK], g, half * 2 + i)
        far_product(g)

    def finish_far(g, i):
        row = rows((1 - half) * 2 + i, BLOCK)
        c = slice(g * BLOCK, (g + 1) * BLOCK)
        quantize(wall[row, c].astype(jnp.float32) + comb[i * BLOCK : (i + 1) * BLOCK, c], g, (1 - half) * 2 + i)

    def far_product(g):
        c = slice(g * BLOCK, (g + 1) * BLOCK)
        comb[:, c] = jnp.dot(ball[rows(1 - half, 256), :], rfv[:, c], preferred_element_type=jnp.float32)

    def ready_far():
        loads[4].wait()
        for k in plane:
            bplane_wait(k, 1)
            scatter_wait(k)
        keep.wait()

    order = ring_order()
    landed = max(e[0] for e in order if e[3] == 0) + 3.5
    todo = [(2.0 + 3.2 * j, functools.partial(hop_step, j)) for j in range(9)]
    todo += [(28.3, spread), (min(landed, 31.0), scatter), (31.0, arrive)]
    todo += [(31.3 + 0.6 * i, functools.partial(squares, NB[0] + i)) for i in range(CHUNKS - NB[0])]
    todo += [(37.6, ready_far)]
    todo += [(37.8 + 0.6 * i, functools.partial(squares, i)) for i in range(NB[0])]
    todo += [(39.8, y_send), (43.0, z_send), (54.0, g_send), (57.5, factors)]
    todo += [(58.0 + 0.5 * g, functools.partial(finish_own, g)) for g in range(CHUNKS)]
    todo += [(64.8 + 0.4 * g, functools.partial(finish_far, g, i)) for g in range(NB[0]) for i in range(2)]
    todo.sort(key=lambda e: e[0])

    for dx in DXS:
        for d in range(2):
            ring_copy(0, 0, lax.rem(x + dx, NX) * 2 + d, d).start()
    own_stage.wait()
    for r in range(1, len(NB)):
        ring_copy(r, 0, me, core).start()
    for i in range(7):
        stage_copy(i).start()
    for i in range(7):
        bplane_copy(i, 0).start()
    for i in range(7):
        own_copy(i).start()
    ps[...] = jnp.zeros_like(ps)
    scv[...] = jnp.zeros_like(scv)

    for now, s, dx, r in order:
        if todo and todo[0][0] <= now:
            todo.pop(0)[1]()
        if s == 0 and r == 0:
            continue
        if s == 0:
            staged_by(dx)
        if s == 0 and dx == 0:
            ring_copy(r, 0, x * 2 + 1 - core, 1 - core).start()
            continue
        for d in range(2):
            k = (dx if s == HOPS - 1 and r > 0 else lax.rem(x + dx, NX)) * 2 + d
            if s > 0:
                ring_wait(r, s - 1, k)
            ring_copy(r, s, k, d).start()
    for _, task in todo:
        task()

    for r in range(1, len(NB)):
        for i in range(2):
            for k in range(4 * i, 4 * i + 4):
                ring_wait(r, HOPS - 1, k)
            for j in range(NB[r]):
                finish_far(C0[r] + j, i)

    scales[...] = scv[0:4, 0:CHUNKS]
    remote(rb, rb, ring_s.at[0], ring_r.at[0, 0, 0], up).wait_send()
    for n, part in enumerate((wall.at[pl.ds(0, 7 * ROWS), rest], wall.at[pl.ds(0, 7 * ROWS), :])):
        remote(part, part, pl_s.at[n], own_r.at[0], up).wait_send()
    for s in range(HOPS):
        for d in range(2):
            bring_copy(s, d).wait_send()
    for i in range(7):
        scatter_copy(i).wait_send()
        for which in range(2):
            bplane_copy(i, which).wait_send()
    for d in range(2):
        chain(d, False).wait_send()
    for i in range(3):
        share_copy(i).wait_send()
        y_copy(i).wait_send()
        g_copy(i).wait_send()
    for i in range(15):
        z_copy(i).wait_send()


def put(result, scales, out, out_scales, sems):
    copies = [pltpu.make_async_copy(scales, out_scales, sems.at[4])]
    for i in range(4):
        part = pl.ds(i * BLOCK, BLOCK)
        copies.append(pltpu.make_async_copy(result.at[part, :], out.at[part, :], sems.at[i]))
    for c in copies:
        c.start()
    for c in copies:
        c.wait()


def body(base_weight, left_factor, right_factor, magnitude):
    bf, f32 = jnp.bfloat16, jnp.float32
    dma = pltpu.SemaphoreType.DMA
    nb = len(NB)
    anywhere = pl.BlockSpec(memory_space=pl.ANY)
    result, scales = pl.pallas_call(
        kernel,
        name="merge",
        out_shape=(
            pltpu.VMEM((16 * ROWS, COLS), bf),
            pltpu.VMEM((4, CHUNKS), f32),
        ),
        in_specs=[anywhere] * 4,
        out_specs=(pl.BlockSpec(memory_space=pltpu.VMEM),) * 2,
        scratch_shapes=[
            pltpu.VMEM((16 * ROWS, COLS), bf),
            pltpu.VMEM((HOPS, PLANE * ROWS, COLS), bf),
            pltpu.VMEM((16 * ROWS, 64), bf),
            pltpu.VMEM((HOPS, ROWS, 64), bf),
            pltpu.VMEM((64, COLS), bf),
            pltpu.VMEM((64, COLS), bf),
            pltpu.VMEM((208, BLOCK), f32),
            pltpu.VMEM((16, BLOCK), f32),
            pltpu.VMEM((8 * ROWS, COLS), f32),
            pltpu.VMEM((NY, 2, 4, BLOCK), f32),
            pltpu.VMEM((NY, 2, 4, BLOCK), f32),
            pltpu.VMEM((2, 4, BLOCK), f32),
            pltpu.VMEM((NZ, 4, BLOCK), f32),
            pltpu.VMEM((NY, 4, BLOCK), f32),
            pltpu.VMEM((8, BLOCK), f32),
            dma((1,)),
            dma((nb, HOPS, PLANE)),
            dma((HOPS, 2)),
            dma((HOPS, 2)),
            dma((2,)),
            dma((PLANE,)),
            dma((PLANE,)),
            dma((2, 7)),
            dma((2, PLANE)),
            dma((2,)),
            dma((2,)),
            dma((3,)),
            dma((NY,)),
            dma((3,)),
            dma((NY,)),
            dma((15,)),
            dma((NZ,)),
            dma((3,)),
            dma((NY,)),
            dma((7,)),
            dma((PLANE,)),
            dma((7,)),
        ],
        compiler_params=pltpu.CompilerParams(collective_id=0, has_side_effects=True),
    )(base_weight, left_factor, right_factor, magnitude.reshape(208, BLOCK))
    return pl.pallas_call(
        put,
        name="put",
        out_shape=(
            jax.ShapeDtypeStruct((16 * ROWS, COLS), bf),
            jax.ShapeDtypeStruct((4, CHUNKS), f32),
        ),
        in_specs=[pl.BlockSpec(memory_space=pltpu.VMEM)] * 2,
        out_specs=(anywhere, anywhere),
        scratch_shapes=[dma((5,))],
    )(*(pltpu.with_memory_space_constraint(v, pltpu.VMEM) for v in (result, scales)))


def solution(mesh):
    in_specs = (P(("fsdp", "tp"), None), P(("fsdp", "tp"), None), P(None, "tp"), P())
    out_specs = (P("fsdp", "tp"), P("fsdp", "tp"))
    return jax.shard_map(body, mesh=mesh, in_specs=in_specs, out_specs=out_specs, check_vma=False)
```
